256 devices in a mesh: cuts: 32 (over z_lo, y, core), coil: 8 (over z_hi, x).
Axes of the slice: x: 4, y: 4, z: 8 (z_hi: 2, z_lo: 4; z = z_hi * 4 + z_lo), core: 2. Of those that a mesh axis runs over, the one named last changes fastest.
Arguments:
- volume: bfloat16 [2, 256, 256, 256], P(None, 'cuts', 'coil'), may hold values from -6 to 6
- coil_maps: bfloat16 [16, 2, 256, 256, 256], P('coil', None, 'cuts'), may hold values from -3 to 3
- kspace: bfloat16 [16, 2, 256, 256, 256], P('coil', None, None, 'cuts'), may hold values from -3 to 3
- line_mask: int32 [256, 256], replicated, may hold values 0 or 1
Outputs:
- updated: bfloat16 [2, 256, 256, 256], P(None, 'coil', 'cuts')
The draws below stay inside these ranges and needn't reach their ends.
All inputs are finite; a program needn't handle non-finite values.
Results may differ from the reference program's by a relative error of at most 0.012.
Values may be sent and summed in bfloat16 or wider, within the bound.
A program may use at most 128 MiB of HBM per device.

```python
import math
import jax
import jax.numpy as jnp
from jax import lax

EDGE = 256
COILS = 16


def touch_ends(drawn, rng, least, largest):
    spot = [jax.random.randint(jax.random.fold_in(rng, axis), (), 0, length) for axis, length in enumerate(drawn.shape)]
    widest = drawn.shape.index(max(drawn.shape))
    next_to = spot[:widest] + [(spot[widest] + 1) % drawn.shape[widest]] + spot[widest + 1:]
    return drawn.at[tuple(spot)].set(least).at[tuple(next_to)].set(largest)


def levels(key, shape, shards, smallest, high):
    def one(axis_at, parts):
        draws = jax.random.uniform(jax.random.fold_in(jax.random.fold_in(key, 6), axis_at), (parts,), jnp.float32, smallest / len(shards), high / len(shards))
        return jnp.repeat(jnp.exp(draws), shape[axis_at] // parts).reshape((-1,) + (1,) * (len(shape) - axis_at - 1))

    loudness = one(*shards[0])
    for cut in shards[1:]:
        loudness = loudness * one(*cut)
    return loudness


def bell_draw(stream_key, extent, width, limit, pieces=(), kind=jnp.bfloat16):
    entries = jax.random.normal(stream_key, extent, jnp.float32) * width
    if len(pieces) > 0:
        entries = levels(stream_key, extent, pieces, -0.22, 0.18) * entries
    return jnp.clip(entries, min=-limit, max=limit).astype(kind)


def setup_inputs(seed: int = 0) -> dict:
    splits = jax.random.split(jax.random.key(seed), 5)
    volume = bell_draw(splits[0], (2, EDGE, EDGE, EDGE), 1.0, 6.0, ((1, 32), (2, 8)))
    coil_maps = bell_draw(splits[1], (COILS, 2, EDGE, EDGE, EDGE), 0.5, 3.0, ((0, 8), (2, 32)))
    kspace = bell_draw(splits[2], (COILS, 2, EDGE, EDGE, EDGE), 0.5, 3.0, ((0, 8), (3, 32)))
    line_mask = touch_ends((jax.random.randint(splits[3], (EDGE, EDGE), 0, 2) < 1).astype(jnp.int32), jax.random.fold_in(splits[3], 1), 0, 1)
    return dict(volume=volume, coil_maps=coil_maps, kspace=kspace, line_mask=line_mask)


def tables(length):
    counter = jnp.arange(length, dtype=jnp.int32)
    product = counter[:, None] * counter[None, :] % length
    angles = product.astype(jnp.float32) * (2.0 * math.pi / length)
    factor = 1.0 / math.sqrt(length)
    return ((jnp.cos(angles) * factor).astype(jnp.bfloat16), (jnp.sin(angles) * factor).astype(jnp.bfloat16))

def contract(pattern, values, table):
    return jnp.einsum(pattern, values.astype(jnp.float32), table.astype(jnp.float32), precision=lax.Precision.HIGHEST)

def transform(real_part, imag_part, cos_table, sin_table, pattern, inverse):
    real_cos = contract(pattern, real_part, cos_table)
    real_sin = contract(pattern, real_part, sin_table)
    imag_cos = contract(pattern, imag_part, cos_table)
    imag_sin = contract(pattern, imag_part, sin_table)
    if inverse:
        return ((real_cos - imag_sin).astype(jnp.bfloat16), (imag_cos + real_sin).astype(jnp.bfloat16))
    return ((real_cos + imag_sin).astype(jnp.bfloat16), (imag_cos - real_sin).astype(jnp.bfloat16))

def reference(volume, coil_maps, kspace, line_mask):
    cos_table, sin_table = tables(EDGE)
    sampled = line_mask.astype(jnp.float32)
    vol_real = volume[0].astype(jnp.float32)
    vol_imag = volume[1].astype(jnp.float32)

    def one_coil(carry, pair):
        maps_one, data_one = pair
        map_real = maps_one[0].astype(jnp.float32)
        map_imag = maps_one[1].astype(jnp.float32)
        coil_real = (map_real * vol_real - map_imag * vol_imag).astype(jnp.bfloat16)
        coil_imag = (map_real * vol_imag + map_imag * vol_real).astype(jnp.bfloat16)
        z_real, z_imag = transform(coil_real, coil_imag, cos_table, sin_table, 'xyn,nk->xyk', False)
        k_real, k_imag = transform(z_real, z_imag, cos_table, sin_table, 'xnz,nk->xkz', False)
        h_real, h_imag = transform(data_one[0], data_one[1], cos_table, sin_table, 'nyz,nk->kyz', True)
        res_real = (sampled * (k_real.astype(jnp.float32) - h_real.astype(jnp.float32))).astype(jnp.bfloat16)
        res_imag = (sampled * (k_imag.astype(jnp.float32) - h_imag.astype(jnp.float32))).astype(jnp.bfloat16)
        y_real, y_imag = transform(res_real, res_imag, cos_table, sin_table, 'xnz,nk->xkz', True)
        b_real, b_imag = transform(y_real, y_imag, cos_table, sin_table, 'xyn,nk->xyk', True)
        back_real = b_real.astype(jnp.float32)
        back_imag = b_imag.astype(jnp.float32)
        grad_real = map_real * back_real + map_imag * back_imag
        grad_imag = map_real * back_imag - map_imag * back_real
        return (carry + jnp.stack([grad_real, grad_imag]), None)
    start = jnp.zeros((2, EDGE, EDGE, EDGE), jnp.float32)
    gradient, _ = lax.scan(one_coil, start, (coil_maps, kspace))
    return (volume.astype(jnp.float32) - 0.5 * gradient).astype(jnp.bfloat16)
```

```python
import functools
import math

import jax
import jax.numpy as jnp
import numpy as np
from jax import lax
from jax.experimental import pallas as pl
from jax.experimental.pallas import tpu as pltpu
from jax.sharding import PartitionSpec as P

MESH = pl.DeviceIdType.MESH
BF16 = jnp.bfloat16
F32 = jnp.float32
N = 256
CUTS = 32
PLANES = 8
GROUPS = 4
XP = PLANES // GROUPS


def tables():
    counter = np.arange(N, dtype=np.int32)
    product = counter[:, None] * counter[None, :] % N
    angles = product.astype(np.float32) * np.float32(2.0 * math.pi / N)
    factor = np.float32(1.0 / math.sqrt(N))
    return (
        (np.cos(angles) * factor).astype(BF16),
        (np.sin(angles) * factor).astype(BF16),
    )


def dot(a, b):
    return jnp.dot(a, b, preferred_element_type=F32)


def kernel(
    vol_in, maps_in, ks_in, mask_in, cos_in, sin_in, out,
    ks, maps, mask, vol, cosv, sinv, fwd, inv, split, merge, hyb, arr, kspc, gsend, rsbuf, psend, fin,
    in_sem, vol_sem, agz_recv, agx_recv, ag_send, a2a_send, a2a_recv, rs_send, rs_recv, mv_send, mv_recv, mv_loc,
):
    me = lax.axis_index("cuts")
    my_coil = lax.axis_index("coil")
    zhi = lax.div(my_coil, 4)
    xpos = lax.rem(my_coil, 4)
    partner = lax.rem(my_coil + 4, 8)
    home = lax.div(me, 4)
    slot = lax.rem(me, 4)

    def load(k, src, dst):
        return pltpu.make_async_copy(src, dst, in_sem.at[k])

    loads = [
        load(0, cos_in, cosv),
        load(1, sin_in, sinv),
        load(2, ks_in.at[0], ks.at[0]),
        load(3, ks_in.at[1], ks.at[1]),
        load(4, mask_in, mask),
        load(5, maps_in, maps),
    ]
    for item in loads:
        item.start()
    my_rows = pl.ds(pl.multiple_of(my_coil * 32, 32), 32)
    vol_own = pltpu.make_async_copy(vol_in, vol.at[:, :, my_rows, :], vol_sem)
    vol_own.start()

    barrier = pltpu.get_barrier_semaphore()

    def greet(a, b):
        pl.semaphore_signal(barrier, inc=1, device_id=(a, b), device_id_type=MESH)

    def greet_cut(k, carry):
        greet(lax.rem(me + k, CUTS), my_coil)
        return carry

    lax.fori_loop(1, CUTS, greet_cut, 0)
    greet(me, partner)
    for d in range(1, 4):
        greet(me, zhi * 4 + lax.rem(xpos + d, 4))
    quarter = lax.div(me, 8)

    def greet_source(k, carry):
        a = my_coil * 4 + lax.rem(k, 4)
        b = lax.div(k, 4) * 4 + quarter

        @pl.when(jnp.logical_or(a != me, b != my_coil))
        def _():
            greet(a, b)

        return carry

    lax.fori_loop(0, 8, greet_source, 0)

    loads[0].wait()
    loads[1].wait()
    c = cosv[...]
    s = sinv[...]
    fwd[:N, :N] = c
    fwd[N:, N:] = c
    fwd[:N, N:] = -s
    fwd[N:, :N] = s
    inv[:N, :N] = c
    inv[N:, N:] = c
    inv[:N, N:] = s
    inv[N:, :N] = -s

    def transform_x(coil):
        for part in range(2):

            def spread(b, carry):
                v = ks[coil, part, pl.ds(pl.multiple_of(b * 32, 32), 32)].astype(F32).reshape(N, N)
                rows = pl.ds(pl.multiple_of(b * N, N), N)
                split[part, 0, rows, :] = v[:, :128]
                split[part, 1, rows, :] = v[:, 128:]
                return carry

            lax.fori_loop(0, 8, spread, 0)

        def line(ky, carry):
            rows = pl.ds(ky, N, stride=8)
            cols = [
                jnp.concatenate([split[0, half, rows, :], split[1, half, rows, :]], axis=0).astype(BF16)
                for half in range(2)
            ]
            r = dot(fwd[...], jnp.concatenate(cols, axis=1))
            for part in range(2):
                for half in range(2):
                    merge[part, half, rows, :] = r[part * N : (part + 1) * N, half * 128 : (half + 1) * 128]
            return carry

        lax.fori_loop(0, 8, line, 0)
        for part in range(2):

            def gather(b, carry):
                rows = pl.ds(pl.multiple_of(b * N, N), N)
                v = jnp.concatenate([merge[part, 0, rows, :], merge[part, 1, rows, :]], axis=1)
                hyb[coil, part, pl.ds(pl.multiple_of(b * 32, 32), 32)] = v.reshape(32, 8, N).astype(BF16)
                return carry

            lax.fori_loop(0, 8, gather, 0)

    def send_slabs(coil, group):
        planes = pl.ds(group * XP, XP)

        def one(k, carry):
            to = lax.rem(me + k, CUTS)
            pltpu.make_async_remote_copy(
                src_ref=hyb.at[coil, :, pl.ds(to * PLANES + group * XP, XP), :, :],
                dst_ref=arr.at[coil, :, planes, me, :, :],
                send_sem=a2a_send.at[group],
                recv_sem=a2a_recv.at[group],
                device_id=(to, my_coil),
                device_id_type=MESH,
            ).start()
            return carry

        lax.fori_loop(1, CUTS, one, 0)
        pltpu.make_async_copy(
            hyb.at[coil, :, pl.ds(me * PLANES + group * XP, XP), :, :],
            arr.at[coil, :, planes, me, :, :],
            a2a_recv.at[group],
        ).start()

    def send_volume(rows, source, peer, recv):
        pltpu.make_async_remote_copy(
            src_ref=source,
            dst_ref=vol.at[:, :, rows, :],
            send_sem=ag_send,
            recv_sem=recv,
            device_id=(me, peer),
            device_id_type=MESH,
        ).start()

    loads[2].wait()
    transform_x(0)
    pl.semaphore_wait(barrier, 43 - self_count(me, my_coil))

    send_volume(my_rows, vol_in, partner, agz_recv)
    for d in range(1, 4):
        send_volume(my_rows, vol_in, zhi * 4 + lax.rem(xpos + d, 4), agx_recv)
    send_slabs(0, 0)
    loads[3].wait()
    transform_x(1)
    send_slabs(1, 0)
    pltpu.make_async_copy(vol_in, vol_in, agz_recv).wait()
    far_rows = pl.ds(pl.multiple_of(partner * 32, 32), 32)
    for d in range(1, 4):
        send_volume(far_rows, vol.at[:, :, far_rows, :], zhi * 4 + lax.rem(xpos + d, 4), agx_recv)
    for group in range(1, GROUPS):
        send_slabs(0, group)
        send_slabs(1, group)

    loads[5].wait()
    vol_own.wait()
    six = vol.at[:, :, pl.ds(0, 192), :]
    pltpu.make_async_copy(six, six, agx_recv).wait()

    def predict(t, carry):
        coil = lax.div(t, PLANES)
        x = lax.rem(t, PLANES)
        vr = vol[0, x].astype(F32)
        vi = vol[1, x].astype(F32)
        mr = maps[coil, 0, x].astype(F32)
        mi = maps[coil, 1, x].astype(F32)
        image = jnp.concatenate([(mr * vr - mi * vi).astype(BF16), (mr * vi + mi * vr).astype(BF16)], axis=1)
        z = dot(image, fwd[...]).astype(BF16)
        kspc[coil, x] = dot(inv[...], jnp.concatenate([z[:, :N], z[:, N:]], axis=0)).astype(BF16)
        return carry

    lax.fori_loop(0, 2 * PLANES, predict, 0)
    loads[4].wait()

    def back(x, carry):
        weight = mask[...].astype(F32)
        gr = None
        for coil in range(2):
            res = []
            for part in range(2):
                k = kspc[coil, x, part * N : (part + 1) * N, :].astype(F32)
                h = arr[coil, part, x].astype(F32).reshape(N, N)
                res.append((weight * (k - h)).astype(BF16))
            y = dot(fwd[...], jnp.concatenate(res, axis=0)).astype(BF16)
            b = dot(jnp.concatenate([y[:N], y[N:]], axis=1), inv[...]).astype(BF16).astype(F32)
            br, bi = b[:, :N], b[:, N:]
            mr = maps[coil, 0, x].astype(F32)
            mi = maps[coil, 1, x].astype(F32)
            tr = mr * br + mi * bi
            ti = mr * bi - mi * br
            gr, gi = (tr, ti) if gr is None else (gr + tr, gi + ti)
        gsend[0, x] = (-0.5 * gr).astype(BF16)
        gsend[1, x] = (-0.5 * gi).astype(BF16)
        return carry

    def send_sums(group):
        planes = pl.ds(group * XP, XP)
        for d in range(1, 4):
            to = lax.rem(xpos + d, 4)
            pltpu.make_async_remote_copy(
                src_ref=gsend.at[:, planes, pl.ds(pl.multiple_of(to * 64, 64), 64), :],
                dst_ref=rsbuf.at[xpos, :, planes, :, :],
                send_sem=rs_send.at[group],
                recv_sem=rs_recv.at[group],
                device_id=(me, zhi * 4 + to),
                device_id_type=MESH,
            ).start()

    lead = (1 - zhi).astype(F32)
    own_rows = pl.ds(pl.multiple_of(xpos * 64, 64), 64)

    def finish_sums(group):
        three = rsbuf.at[pl.ds(0, 3), :, pl.ds(group * XP, XP), :, :]
        pltpu.make_async_copy(three, three, rs_recv.at[group]).wait()

        def one(t, carry):
            part = lax.rem(t, 2)
            x = group * XP + lax.div(t, 2)
            total = lead * vol[part, x, own_rows, :].astype(F32) + gsend[part, x, own_rows, :].astype(F32)
            for d in range(1, 4):
                total += rsbuf[lax.rem(xpos + d, 4), part, x].astype(F32)
            psend[part, x] = total.reshape(8, 8, N).astype(BF16)
            return carry

        lax.fori_loop(0, 2 * XP, one, 0)

        def move(k, carry):
            to = xpos * 8 + k
            src = psend.at[:, pl.ds(group * XP, XP), k, :, :]
            dst = fin.at[zhi, :, pl.ds(slot * PLANES + group * XP, XP), :, :]
            itself = jnp.logical_and(to == me, home == my_coil)

            @pl.when(itself)
            def _():
                pltpu.make_async_copy(src, dst, mv_loc.at[group]).start()

            @pl.when(jnp.logical_not(itself))
            def _():
                pltpu.make_async_remote_copy(
                    src_ref=src,
                    dst_ref=dst,
                    send_sem=mv_send.at[group],
                    recv_sem=mv_recv.at[group],
                    device_id=(to, home),
                    device_id_type=MESH,
                ).start()

            return carry

        lax.fori_loop(0, 8, move, 0)

    for group in range(GROUPS):
        here = arr.at[:, :, pl.ds(group * XP, XP), :, :, :]
        pltpu.make_async_copy(here, here, a2a_recv.at[group]).wait()
        lax.fori_loop(group * XP, (group + 1) * XP, back, 0)
        send_sums(group)
        if group > 0:
            finish_sums(group - 1)
    finish_sums(GROUPS - 1)

    alone = self_count(me, my_coil) == 1
    for group in range(GROUPS):
        full = psend.at[:, pl.ds(group * XP, XP), :, :, :]
        most = psend.at[:, pl.ds(group * XP, XP), pl.ds(0, 7), :, :]
        single = psend.at[:, pl.ds(group * XP, XP), 0, :, :]

        @pl.when(alone)
        def _():
            pltpu.make_async_copy(most, most, mv_recv.at[group]).wait()
            pltpu.make_async_copy(single, single, mv_loc.at[group]).wait()
            pltpu.make_async_copy(most, most, mv_send.at[group]).wait()

        @pl.when(jnp.logical_not(alone))
        def _():
            pltpu.make_async_copy(full, full, mv_recv.at[group]).wait()
            pltpu.make_async_copy(full, full, mv_send.at[group]).wait()

    for part in range(2):
        out[part] = (fin[0, part].astype(F32) + fin[1, part].astype(F32)).astype(BF16)

    for group in range(GROUPS):
        sent = hyb.at[:, :, pl.ds(0, 31 * XP), :, :]
        pltpu.make_async_copy(sent, sent, a2a_send.at[group]).wait()
        three = rsbuf.at[pl.ds(0, 3), :, pl.ds(group * XP, XP), :, :]
        pltpu.make_async_copy(three, three, rs_send.at[group]).wait()
    seven = vol.at[:, :, pl.ds(0, 224), :]
    pltpu.make_async_copy(seven, seven, ag_send).wait()


def self_count(me, my_coil):
    same = jnp.logical_and(lax.div(me, 8) == lax.rem(my_coil, 4), lax.div(me, 4) == my_coil)
    return same.astype(jnp.int32)


def body(volume, coil_maps, kspace, line_mask):
    cos_table, sin_table = tables()
    any_space = pl.BlockSpec(memory_space=pl.ANY)
    dma = pltpu.SemaphoreType.DMA
    return pl.pallas_call(
        kernel,
        out_shape=jax.ShapeDtypeStruct((2, 32, 8, N), BF16),
        in_specs=[any_space] * 6,
        out_specs=pl.BlockSpec(memory_space=pltpu.VMEM),
        scratch_shapes=[
            pltpu.VMEM((2, 2, N, 8, N), BF16),
            pltpu.VMEM((2, 2, PLANES, N, N), BF16),
            pltpu.VMEM((N, N), jnp.int32),
            pltpu.VMEM((2, PLANES, N, N), BF16),
            pltpu.VMEM((N, N), BF16),
            pltpu.VMEM((N, N), BF16),
            pltpu.VMEM((2 * N, 2 * N), BF16),
            pltpu.VMEM((2 * N, 2 * N), BF16),
            pltpu.VMEM((2, 2, 8 * N, 128), F32),
            pltpu.VMEM((2, 2, 8 * N, 128), F32),
            pltpu.VMEM((2, 2, N, 8, N), BF16),
            pltpu.VMEM((2, 2, PLANES, CUTS, 8, N), BF16),
            pltpu.VMEM((2, PLANES, 2 * N, N), BF16),
            pltpu.VMEM((2, PLANES, N, N), BF16),
            pltpu.VMEM((4, 2, PLANES, 64, N), BF16),
            pltpu.VMEM((2, PLANES, 8, 8, N), BF16),
            pltpu.VMEM((2, 2, 32, 8, N), BF16),
            dma((6,)),
            dma,
            dma,
            dma,
            dma,
            dma((GROUPS,)),
            dma((GROUPS,)),
            dma((GROUPS,)),
            dma((GROUPS,)),
            dma((GROUPS,)),
            dma((GROUPS,)),
            dma((GROUPS,)),
        ],
        compiler_params=pltpu.CompilerParams(
            collective_id=0, has_side_effects=True, vmem_limit_bytes=60 * 1024 * 1024
        ),
    )(volume, coil_maps, kspace, line_mask, jnp.asarray(cos_table), jnp.asarray(sin_table))


def solution(mesh):
    return jax.shard_map(
        body,
        mesh=mesh,
        in_specs=(
            P(None, "cuts", "coil", None),
            P("coil", None, "cuts", None, None),
            P("coil", None, None, "cuts", None),
            P(),
        ),
        out_specs=P(None, "coil", "cuts", None),
        check_vma=False,
    )
```

```python
import math

import jax
import jax.numpy as jnp
import numpy as np
from jax import lax
from jax.experimental import pallas as pl
from jax.experimental.pallas import tpu as pltpu
from jax.sharding import PartitionSpec as P

MESH = pl.DeviceIdType.MESH
BF16 = jnp.bfloat16
F32 = jnp.float32
N = 256
CUTS = 32
PLANES = 8
SIZES = (2, 2, 2, 1, 1)
GROUPS = len(SIZES)
FIRST = tuple(sum(SIZES[:g]) for g in range(GROUPS))


def tables():
    counter = np.arange(N, dtype=np.int32)
    product = counter[:, None] * counter[None, :] % N
    angles = product.astype(np.float32) * np.float32(2.0 * math.pi / N)
    factor = np.float32(1.0 / math.sqrt(N))
    return (
        (np.cos(angles) * factor).astype(BF16),
        (np.sin(angles) * factor).astype(BF16),
    )


def dot(a, b):
    return jnp.dot(a, b, preferred_element_type=F32)


def kernel(
    vol_in, maps_in, ks_in, mask_in, cos_in, sin_in, out,
    ks, maps, mask, vol, cosv, sinv, fwd, inv, split, merge, hyb, arr, kspc, gsend, rsbuf, psend, mid, osend, fin,
    in_sem, vol_sem, agz_recv, agx_recv, ag_send, a2a_send, a2a_recv, rs_send, rs_recv, mid_send, mid_recv, mv_send, mv_recv, out_sem,
):
    me = lax.axis_index("cuts")
    my_coil = lax.axis_index("coil")
    zhi = lax.div(my_coil, 4)
    xpos = lax.rem(my_coil, 4)
    partner = lax.rem(my_coil + 4, 8)
    zlo = lax.div(me, 8)
    ypos = lax.rem(lax.div(me, 2), 4)
    core = lax.rem(me, 2)
    slot = lax.rem(me, 4)
    shift = lax.rem(zlo + 2 * core, 4)
    quarter = lax.rem(xpos + shift, 4)
    mid_cut = quarter * 8 + lax.rem(me, 8)
    mid_coil = lax.div(zlo, 2) * 4 + xpos
    stays = jnp.logical_and(mid_cut == me, mid_coil == my_coil)
    zlo_from = lax.rem(zlo + 8 - xpos - 2 * core, 4)
    is_mid = lax.div(zlo_from, 2) == zhi
    owner_coil = zlo_from * 2 + lax.div(ypos, 2)
    keeps = owner_coil == my_coil
    zlo_home = 2 * zhi + lax.div(xpos, 2)

    def load(k, src, dst):
        return pltpu.make_async_copy(src, dst, in_sem.at[k])

    loads = [
        load(0, cos_in, cosv),
        load(1, sin_in, sinv),
        load(2, ks_in.at[0], ks.at[0]),
        load(3, ks_in.at[1], ks.at[1]),
        load(4, mask_in, mask),
        load(5, maps_in, maps),
    ]
    for item in loads:
        item.start()
    my_rows = pl.ds(pl.multiple_of(my_coil * 32, 32), 32)
    vol_own = pltpu.make_async_copy(vol_in, vol.at[:, :, my_rows, :], vol_sem)
    vol_own.start()

    barrier = pltpu.get_barrier_semaphore()

    def greet(a, b):
        pl.semaphore_signal(barrier, inc=1, device_id=(a, b), device_id_type=MESH)

    def greet_cut(k, carry):
        greet(lax.rem(me + k, CUTS), my_coil)
        return carry

    lax.fori_loop(1, CUTS, greet_cut, 0)
    greet(me, partner)
    for d in range(1, 4):
        greet(me, zhi * 4 + lax.rem(xpos + d, 4))

    @pl.when(is_mid)
    def _():
        for z in range(2):
            a, b = zlo_from * 8 + lax.rem(me, 8), z * 4 + xpos

            @pl.when(jnp.logical_or(a != me, b != my_coil))
            def _():
                greet(a, b)

    for m in range(4):
        a = zlo * 8 + lax.rem(xpos, 2) * 4 + m
        b = zhi * 4 + lax.rem(zlo + 8 - zlo_home - 2 * (m % 2), 4)

        @pl.when(jnp.logical_or(a != me, b != my_coil))
        def _():
            greet(a, b)

    loads[0].wait()
    loads[1].wait()
    c = cosv[...]
    s = sinv[...]
    fwd[:N, :N] = c
    fwd[N:, N:] = c
    fwd[:N, N:] = -s
    fwd[N:, :N] = s
    inv[:N, :N] = c
    inv[N:, N:] = c
    inv[:N, N:] = s
    inv[N:, :N] = -s

    def transform_x(coil):
        for part in range(2):

            def spread(b, carry):
                v = ks[coil, part, pl.ds(pl.multiple_of(b * 32, 32), 32)].astype(F32).reshape(N, N)
                rows = pl.ds(pl.multiple_of(b * N, N), N)
                split[part, 0, rows, :] = v[:, :128]
                split[part, 1, rows, :] = v[:, 128:]
                return carry

            lax.fori_loop(0, 8, spread, 0)

        def line(ky, carry):
            rows = pl.ds(ky, N, stride=8)
            cols = [
                jnp.concatenate([split[0, half, rows, :], split[1, half, rows, :]], axis=0).astype(BF16)
                for half in range(2)
            ]
            r = dot(fwd[...], jnp.concatenate(cols, axis=1))
            for part in range(2):
                for half in range(2):
                    merge[part, half, rows, :] = r[part * N : (part + 1) * N, half * 128 : (half + 1) * 128]
            return carry

        lax.fori_loop(0, 8, line, 0)
        for part in range(2):

            def gather(b, carry):
                rows = pl.ds(pl.multiple_of(b * N, N), N)
                v = jnp.concatenate([merge[part, 0, rows, :], merge[part, 1, rows, :]], axis=1)
                hyb[coil, part, pl.ds(pl.multiple_of(b * 32, 32), 32)] = v.reshape(32, 8, N).astype(BF16)
                return carry

            lax.fori_loop(0, 8, gather, 0)

    def send_slabs(coil, group):
        planes = pl.ds(FIRST[group], SIZES[group])

        def one(k, carry):
            to = lax.rem(me + k, CUTS)
            pltpu.make_async_remote_copy(
                src_ref=hyb.at[coil, :, pl.ds(to * PLANES + FIRST[group], SIZES[group]), :, :],
                dst_ref=arr.at[coil, :, planes, me, :, :],
                send_sem=a2a_send.at[group],
                recv_sem=a2a_recv.at[group],
                device_id=(to, my_coil),
                device_id_type=MESH,
            ).start()
            return carry

        lax.fori_loop(1, CUTS, one, 0)
        pltpu.make_async_copy(
            hyb.at[coil, :, pl.ds(me * PLANES + FIRST[group], SIZES[group]), :, :],
            arr.at[coil, :, planes, me, :, :],
            a2a_recv.at[group],
        ).start()

    def send_volume(rows, source, peer, recv):
        pltpu.make_async_remote_copy(
            src_ref=source,
            dst_ref=vol.at[:, :, rows, :],
            send_sem=ag_send,
            recv_sem=recv,
            device_id=(me, peer),
            device_id_type=MESH,
        ).start()

    loads[2].wait()
    transform_x(0)
    greeted = jnp.where(is_mid, 8 - keeps.astype(jnp.int32), 0) + 1 - stays.astype(jnp.int32)
    pl.semaphore_wait(barrier, 35 + greeted)

    send_volume(my_rows, vol_in, partner, agz_recv)
    for d in range(1, 4):
        send_volume(my_rows, vol_in, zhi * 4 + lax.rem(xpos + d, 4), agx_recv)
    send_slabs(0, 0)
    loads[3].wait()
    transform_x(1)
    send_slabs(1, 0)
    pltpu.make_async_copy(vol_in, vol_in, agz_recv).wait()
    far_rows = pl.ds(pl.multiple_of(partner * 32, 32), 32)
    for d in range(1, 4):
        send_volume(far_rows, vol.at[:, :, far_rows, :], zhi * 4 + lax.rem(xpos + d, 4), agx_recv)
    for group in range(1, GROUPS):
        send_slabs(0, group)
        send_slabs(1, group)

    loads[5].wait()
    vol_own.wait()
    six = vol.at[:, :, pl.ds(0, 192), :]
    pltpu.make_async_copy(six, six, agx_recv).wait()

    def predict(t, carry):
        coil = lax.div(t, PLANES)
        x = lax.rem(t, PLANES)
        vr = vol[0, x].astype(F32)
        vi = vol[1, x].astype(F32)
        mr = maps[coil, 0, x].astype(F32)
        mi = maps[coil, 1, x].astype(F32)
        image = jnp.concatenate([(mr * vr - mi * vi).astype(BF16), (mr * vi + mi * vr).astype(BF16)], axis=1)
        z = dot(image, fwd[...]).astype(BF16)
        kspc[coil, x] = dot(inv[...], jnp.concatenate([z[:, :N], z[:, N:]], axis=0)).astype(BF16)
        return carry

    lax.fori_loop(0, 2 * PLANES, predict, 0)
    loads[4].wait()

    def back(x, carry):
        weight = mask[...].astype(F32)
        gr = None
        for coil in range(2):
            res = []
            for part in range(2):
                k = kspc[coil, x, part * N : (part + 1) * N, :].astype(F32)
                h = arr[coil, part, x].astype(F32).reshape(N, N)
                res.append((weight * (k - h)).astype(BF16))
            y = dot(fwd[...], jnp.concatenate(res, axis=0)).astype(BF16)
            b = dot(jnp.concatenate([y[:N], y[N:]], axis=1), inv[...]).astype(BF16).astype(F32)
            br, bi = b[:, :N], b[:, N:]
            mr = maps[coil, 0, x].astype(F32)
            mi = maps[coil, 1, x].astype(F32)
            tr = mr * br + mi * bi
            ti = mr * bi - mi * br
            gr, gi = (tr, ti) if gr is None else (gr + tr, gi + ti)
        gsend[0, x] = (-0.5 * gr).astype(BF16)
        gsend[1, x] = (-0.5 * gi).astype(BF16)
        return carry

    def send_sums(group):
        planes = pl.ds(FIRST[group], SIZES[group])
        for d in range(1, 4):
            to = lax.rem(xpos + d, 4)
            pltpu.make_async_remote_copy(
                src_ref=gsend.at[:, planes, pl.ds(pl.multiple_of(lax.rem(to + shift, 4) * 64, 64), 64), :],
                dst_ref=rsbuf.at[xpos, :, planes, :, :],
                send_sem=rs_send.at[group],
                recv_sem=rs_recv.at[group],
                device_id=(me, zhi * 4 + to),
                device_id_type=MESH,
            ).start()

    lead = (1 - zhi).astype(F32)
    own_rows = pl.ds(pl.multiple_of(quarter * 64, 64), 64)

    def finish_sums(group):
        planes = pl.ds(FIRST[group], SIZES[group])
        three = rsbuf.at[pl.ds(0, 3), :, planes, :, :]
        pltpu.make_async_copy(three, three, rs_recv.at[group]).wait()

        def one(t, carry):
            part = lax.rem(t, 2)
            x = FIRST[group] + lax.div(t, 2)
            total = lead * vol[part, x, own_rows, :].astype(F32) + gsend[part, x, own_rows, :].astype(F32)
            for d in range(1, 4):
                total += rsbuf[lax.rem(xpos + d, 4), part, x].astype(F32)
            psend[part, x] = total.astype(BF16)
            return carry

        lax.fori_loop(0, 2 * SIZES[group], one, 0)
        src = psend.at[:, planes, :, :]
        dst = mid.at[zhi, :, planes, :, :]

        @pl.when(stays)
        def _():
            pltpu.make_async_copy(src, dst, mid_recv.at[group]).start()

        @pl.when(jnp.logical_not(stays))
        def _():
            pltpu.make_async_remote_copy(
                src_ref=src,
                dst_ref=dst,
                send_sem=mid_send.at[group],
                recv_sem=mid_recv.at[group],
                device_id=(mid_cut, mid_coil),
                device_id_type=MESH,
            ).start()

    def move_out(group):
        planes = pl.ds(FIRST[group], SIZES[group])

        @pl.when(is_mid)
        def _():
            both = mid.at[:, :, planes, :, :]
            pltpu.make_async_copy(both, both, mid_recv.at[group]).wait()

            def one(t, carry):
                part = lax.rem(t, 2)
                x = FIRST[group] + lax.div(t, 2)
                total = mid[0, part, x].astype(F32) + mid[1, part, x].astype(F32)
                osend[part, x] = total.reshape(8, 8, N).astype(BF16)
                return carry

            lax.fori_loop(0, 2 * SIZES[group], one, 0)

            def move(k, carry):
                src = osend.at[:, planes, k, :, :]
                dst = fin.at[:, pl.ds(slot * PLANES + FIRST[group], SIZES[group]), :, :]
                itself = jnp.logical_and(keeps, lax.rem(me, 8) == k)

                @pl.when(itself)
                def _():
                    pltpu.make_async_copy(src, dst, mv_recv.at[group]).start()

                @pl.when(jnp.logical_not(itself))
                def _():
                    pltpu.make_async_remote_copy(
                        src_ref=src,
                        dst_ref=dst,
                        send_sem=mv_send.at[group],
                        recv_sem=mv_recv.at[group],
                        device_id=(zlo * 8 + k, owner_coil),
                        device_id_type=MESH,
                    ).start()

                return carry

            lax.fori_loop(0, 8, move, 0)

    for group in range(GROUPS):
        here = arr.at[:, :, pl.ds(FIRST[group], SIZES[group]), :, :, :]
        pltpu.make_async_copy(here, here, a2a_recv.at[group]).wait()
        lax.fori_loop(FIRST[group], FIRST[group] + SIZES[group], back, 0)
        send_sums(group)
        if group > 0:
            finish_sums(group - 1)
        if group > 1:
            move_out(group - 2)
    move_out(GROUPS - 2)
    finish_sums(GROUPS - 1)
    move_out(GROUPS - 1)

    for group in range(GROUPS):
        four = fin.at[:, pl.ds(0, 4 * SIZES[group]), :, :]
        pltpu.make_async_copy(four, four, mv_recv.at[group]).wait()
    result = pltpu.make_async_copy(fin, out, out_sem)
    result.start()

    for group in range(GROUPS):
        planes = pl.ds(FIRST[group], SIZES[group])
        sent = hyb.at[:, :, pl.ds(0, 31 * SIZES[group]), :, :]
        pltpu.make_async_copy(sent, sent, a2a_send.at[group]).wait()
        three = rsbuf.at[pl.ds(0, 3), :, planes, :, :]
        pltpu.make_async_copy(three, three, rs_send.at[group]).wait()

        @pl.when(jnp.logical_not(stays))
        def _():
            part = psend.at[:, planes, :, :]
            pltpu.make_async_copy(part, part, mid_send.at[group]).wait()

        @pl.when(jnp.logical_and(is_mid, keeps))
        def _():
            seven = osend.at[:, planes, pl.ds(0, 7), :, :]
            pltpu.make_async_copy(seven, seven, mv_send.at[group]).wait()

        @pl.when(jnp.logical_and(is_mid, jnp.logical_not(keeps)))
        def _():
            eight = osend.at[:, planes, :, :, :]
            pltpu.make_async_copy(eight, eight, mv_send.at[group]).wait()

    seven = vol.at[:, :, pl.ds(0, 224), :]
    pltpu.make_async_copy(seven, seven, ag_send).wait()
    result.wait()


def body(volume, coil_maps, kspace, line_mask):
    cos_table, sin_table = tables()
    any_space = pl.BlockSpec(memory_space=pl.ANY)
    dma = pltpu.SemaphoreType.DMA
    return pl.pallas_call(
        kernel,
        out_shape=jax.ShapeDtypeStruct((2, 32, 8, N), BF16),
        in_specs=[any_space] * 6,
        out_specs=any_space,
        scratch_shapes=[
            pltpu.VMEM((2, 2, N, 8, N), BF16),
            pltpu.VMEM((2, 2, PLANES, N, N), BF16),
            pltpu.VMEM((N, N), jnp.int32),
            pltpu.VMEM((2, PLANES, N, N), BF16),
            pltpu.VMEM((N, N), BF16),
            pltpu.VMEM((N, N), BF16),
            pltpu.VMEM((2 * N, 2 * N), BF16),
            pltpu.VMEM((2 * N, 2 * N), BF16),
            pltpu.VMEM((2, 2, 8 * N, 128), F32),
            pltpu.VMEM((2, 2, 8 * N, 128), F32),
            pltpu.VMEM((2, 2, N, 8, N), BF16),
            pltpu.VMEM((2, 2, PLANES, CUTS, 8, N), BF16),
            pltpu.VMEM((2, PLANES, 2 * N, N), BF16),
            pltpu.VMEM((2, PLANES, N, N), BF16),
            pltpu.VMEM((4, 2, PLANES, 64, N), BF16),
            pltpu.VMEM((2, PLANES, 64, N), BF16),
            pltpu.VMEM((2, 2, PLANES, 64, N), BF16),
            pltpu.VMEM((2, PLANES, 8, 8, N), BF16),
            pltpu.VMEM((2, 32, 8, N), BF16),
            dma((6,)),
            dma,
            dma,
            dma,
            dma,
            dma((GROUPS,)),
            dma((GROUPS,)),
            dma((GROUPS,)),
            dma((GROUPS,)),
            dma((GROUPS,)),
            dma((GROUPS,)),
            dma((GROUPS,)),
            dma((GROUPS,)),
            dma,
        ],
        compiler_params=pltpu.CompilerParams(
            collective_id=0, has_side_effects=True, vmem_limit_bytes=60 * 1024 * 1024
        ),
    )(volume, coil_maps, kspace, line_mask, jnp.asarray(cos_table), jnp.asarray(sin_table))


def solution(mesh):
    return jax.shard_map(
        body,
        mesh=mesh,
        in_specs=(
            P(None, "cuts", "coil", None),
            P("coil", None, "cuts", None, None),
            P("coil", None, None, "cuts", None),
            P(),
        ),
        out_specs=P(None, "coil", "cuts", None),
        check_vma=False,
    )
```

```python
import math

import jax
import jax.numpy as jnp
import numpy as np
from jax import lax
from jax.experimental import pallas as pl
from jax.experimental.pallas import tpu as pltpu
from jax.sharding import PartitionSpec as P

MESH = pl.DeviceIdType.MESH
BF16 = jnp.bfloat16
F32 = jnp.float32
N = 256
CUTS = 32
PLANES = 8
SIZES = (3, 3, 1, 1)
GROUPS = len(SIZES)
FIRST = tuple(sum(SIZES[:g]) for g in range(GROUPS))


def tables():
    counter = np.arange(N, dtype=np.int32)
    product = counter[:, None] * counter[None, :] % N
    angles = product.astype(np.float32) * np.float32(2.0 * math.pi / N)
    factor = np.float32(1.0 / math.sqrt(N))
    return (
        (np.cos(angles) * factor).astype(BF16),
        (np.sin(angles) * factor).astype(BF16),
    )


def dot(a, b):
    return jnp.dot(a, b, preferred_element_type=F32)


def kernel(
    vol_in, maps_in, ks_in, mask_in, cos_in, sin_in, out,
    ks, maps, mask, vol, cosv, sinv, fwd, inv, split, merge, hyb, arr, kspc, gsend, rsbuf, psend, mid, osend, fin,
    in_sem, vol_sem, agz_recv, agx_recv, ag_send, a2a_send, a2a_recv, rs_send, rs_recv, mid_send, mid_recv, mv_send, mv_recv, out_sem,
):
    me = lax.axis_index("cuts")
    my_coil = lax.axis_index("coil")
    zhi = lax.div(my_coil, 4)
    xpos = lax.rem(my_coil, 4)
    partner = lax.rem(my_coil + 4, 8)
    zlo = lax.div(me, 8)
    ypos = lax.rem(lax.div(me, 2), 4)
    core = lax.rem(me, 2)
    slot = lax.rem(me, 4)
    shift = lax.rem(zlo + 2 * core, 4)
    quarter = lax.rem(xpos + shift, 4)
    mid_cut = quarter * 8 + lax.rem(me, 8)
    mid_coil = lax.div(zlo, 2) * 4 + xpos
    stays = jnp.logical_and(mid_cut == me, mid_coil == my_coil)
    zlo_from = lax.rem(zlo + 8 - xpos - 2 * core, 4)
    is_mid = lax.div(zlo_from, 2) == zhi
    owner_coil = zlo_from * 2 + lax.div(ypos, 2)
    keeps = owner_coil == my_coil
    zlo_home = 2 * zhi + lax.div(xpos, 2)

    def load(k, src, dst):
        return pltpu.make_async_copy(src, dst, in_sem.at[k])

    loads = [
        load(0, cos_in, cosv),
        load(1, sin_in, sinv),
        load(2, ks_in.at[0], ks.at[0]),
        load(3, ks_in.at[1], ks.at[1]),
        load(4, mask_in, mask),
        load(5, maps_in, maps),
    ]
    for item in loads:
        item.start()
    my_rows = pl.ds(pl.multiple_of(my_coil * 32, 32), 32)
    vol_own = pltpu.make_async_copy(vol_in, vol.at[:, :, my_rows, :], vol_sem)
    vol_own.start()

    barrier = pltpu.get_barrier_semaphore()

    def greet(a, b):
        pl.semaphore_signal(barrier, inc=1, device_id=(a, b), device_id_type=MESH)

    def greet_cut(k, carry):
        greet(lax.rem(me + k, CUTS), my_coil)
        return carry

    lax.fori_loop(1, CUTS, greet_cut, 0)
    greet(me, partner)
    for d in range(1, 4):
        greet(me, zhi * 4 + lax.rem(xpos + d, 4))

    @pl.when(is_mid)
    def _():
        for z in range(2):
            a, b = zlo_from * 8 + lax.rem(me, 8), z * 4 + xpos

            @pl.when(jnp.logical_or(a != me, b != my_coil))
            def _():
                greet(a, b)

    for m in range(4):
        a = zlo * 8 + lax.rem(xpos, 2) * 4 + m
        b = zhi * 4 + lax.rem(zlo + 8 - zlo_home - 2 * (m % 2), 4)

        @pl.when(jnp.logical_or(a != me, b != my_coil))
        def _():
            greet(a, b)

    loads[0].wait()
    loads[1].wait()
    c = cosv[...]
    s = sinv[...]
    fwd[:N, :N] = c
    fwd[N:, N:] = c
    fwd[:N, N:] = -s
    fwd[N:, :N] = s
    inv[:N, :N] = c
    inv[N:, N:] = c
    inv[:N, N:] = s
    inv[N:, :N] = -s

    def transform_x(coil):
        for part in range(2):

            def spread(b, carry):
                v = ks[coil, part, pl.ds(pl.multiple_of(b * 32, 32), 32)].astype(F32).reshape(N, N)
                rows = pl.ds(pl.multiple_of(b * N, N), N)
                split[part, 0, rows, :] = v[:, :128]
                split[part, 1, rows, :] = v[:, 128:]
                return carry

            lax.fori_loop(0, 8, spread, 0)

        def line(ky, carry):
            rows = pl.ds(ky, N, stride=8)
            cols = [
                jnp.concatenate([split[0, half, rows, :], split[1, half, rows, :]], axis=0).astype(BF16)
                for half in range(2)
            ]
            r = dot(fwd[...], jnp.concatenate(cols, axis=1))
            for part in range(2):
                for half in range(2):
                    merge[part, half, rows, :] = r[part * N : (part + 1) * N, half * 128 : (half + 1) * 128]
            return carry

        lax.fori_loop(0, 8, line, 0)
        for part in range(2):

            def gather(b, carry):
                rows = pl.ds(pl.multiple_of(b * N, N), N)
                v = jnp.concatenate([merge[part, 0, rows, :], merge[part, 1, rows, :]], axis=1)
                hyb[coil, part, pl.ds(pl.multiple_of(b * 32, 32), 32)] = v.reshape(32, 8, N).astype(BF16)
                return carry

            lax.fori_loop(0, 8, gather, 0)

    def send_slabs(coil, group):
        planes = pl.ds(FIRST[group], SIZES[group])

        def one(k, carry):
            to = lax.rem(me + k, CUTS)
            pltpu.make_async_remote_copy(
                src_ref=hyb.at[coil, :, pl.ds(to * PLANES + FIRST[group], SIZES[group]), :, :],
                dst_ref=arr.at[coil, :, planes, me, :, :],
                send_sem=a2a_send.at[group],
                recv_sem=a2a_recv.at[group],
                device_id=(to, my_coil),
                device_id_type=MESH,
            ).start()
            return carry

        lax.fori_loop(1, CUTS, one, 0)
        pltpu.make_async_copy(
            hyb.at[coil, :, pl.ds(me * PLANES + FIRST[group], SIZES[group]), :, :],
            arr.at[coil, :, planes, me, :, :],
            a2a_recv.at[group],
        ).start()

    def send_volume(rows, source, peer, recv):
        pltpu.make_async_remote_copy(
            src_ref=source,
            dst_ref=vol.at[:, :, rows, :],
            send_sem=ag_send,
            recv_sem=recv,
            device_id=(me, peer),
            device_id_type=MESH,
        ).start()

    loads[2].wait()
    transform_x(0)
    greeted = jnp.where(is_mid, 8 - keeps.astype(jnp.int32), 0) + 1 - stays.astype(jnp.int32)
    pl.semaphore_wait(barrier, 35 + greeted)

    send_volume(my_rows, vol_in, partner, agz_recv)
    for d in range(1, 4):
        send_volume(my_rows, vol_in, zhi * 4 + lax.rem(xpos + d, 4), agx_recv)
    send_slabs(0, 0)
    loads[3].wait()
    transform_x(1)
    send_slabs(1, 0)
    pltpu.make_async_copy(vol_in, vol_in, agz_recv).wait()
    far_rows = pl.ds(pl.multiple_of(partner * 32, 32), 32)
    for d in range(1, 4):
        send_volume(far_rows, vol.at[:, :, far_rows, :], zhi * 4 + lax.rem(xpos + d, 4), agx_recv)
    for group in range(1, GROUPS):
        send_slabs(0, group)
        send_slabs(1, group)

    loads[5].wait()
    vol_own.wait()
    six = vol.at[:, :, pl.ds(0, 192), :]
    pltpu.make_async_copy(six, six, agx_recv).wait()

    def predict(t, carry):
        coil = lax.div(t, PLANES)
        x = lax.rem(t, PLANES)
        vr = vol[0, x].astype(F32)
        vi = vol[1, x].astype(F32)
        mr = maps[coil, 0, x].astype(F32)
        mi = maps[coil, 1, x].astype(F32)
        image = jnp.concatenate([(mr * vr - mi * vi).astype(BF16), (mr * vi + mi * vr).astype(BF16)], axis=1)
        z = dot(image, fwd[...]).astype(BF16)
        kspc[coil, x] = dot(inv[...], jnp.concatenate([z[:, :N], z[:, N:]], axis=0)).astype(BF16)
        return carry

    lax.fori_loop(0, 2 * PLANES, predict, 0)
    loads[4].wait()

    def back(x, carry):
        weight = mask[...].astype(F32)
        gr = None
        for coil in range(2):
            res = []
            for part in range(2):
                k = kspc[coil, x, part * N : (part + 1) * N, :].astype(F32)
                h = arr[coil, part, x].astype(F32).reshape(N, N)
                res.append((weight * (k - h)).astype(BF16))
            y = dot(fwd[...], jnp.concatenate(res, axis=0)).astype(BF16)
            b = dot(jnp.concatenate([y[:N], y[N:]], axis=1), inv[...]).astype(BF16).astype(F32)
            br, bi = b[:, :N], b[:, N:]
            mr = maps[coil, 0, x].astype(F32)
            mi = maps[coil, 1, x].astype(F32)
            tr = mr * br + mi * bi
            ti = mr * bi - mi * br
            gr, gi = (tr, ti) if gr is None else (gr + tr, gi + ti)
        gsend[0, x] = (-0.5 * gr).astype(BF16)
        gsend[1, x] = (-0.5 * gi).astype(BF16)
        return carry

    def send_sums(group):
        planes = pl.ds(FIRST[group], SIZES[group])
        for d in range(1, 4):
            to = lax.rem(xpos + d, 4)
            pltpu.make_async_remote_copy(
                src_ref=gsend.at[:, planes, pl.ds(pl.multiple_of(lax.rem(to + shift, 4) * 64, 64), 64), :],
                dst_ref=rsbuf.at[xpos, :, planes, :, :],
                send_sem=rs_send.at[group],
                recv_sem=rs_recv.at[group],
                device_id=(me, zhi * 4 + to),
                device_id_type=MESH,
            ).start()

    lead = (1 - zhi).astype(F32)
    own_rows = pl.ds(pl.multiple_of(quarter * 64, 64), 64)

    def finish_sums(group):
        planes = pl.ds(FIRST[group], SIZES[group])
        three = rsbuf.at[pl.ds(0, 3), :, planes, :, :]
        pltpu.make_async_copy(three, three, rs_recv.at[group]).wait()

        def one(t, carry):
            part = lax.rem(t, 2)
            x = FIRST[group] + lax.div(t, 2)
            total = lead * vol[part, x, own_rows, :].astype(F32) + gsend[part, x, own_rows, :].astype(F32)
            for d in range(1, 4):
                total += rsbuf[lax.rem(xpos + d, 4), part, x].astype(F32)
            psend[part, x] = total.astype(BF16)
            return carry

        lax.fori_loop(0, 2 * SIZES[group], one, 0)
        src = psend.at[:, planes, :, :]
        dst = mid.at[zhi, :, planes, :, :]

        @pl.when(stays)
        def _():
            pltpu.make_async_copy(src, dst, mid_recv.at[group]).start()

        @pl.when(jnp.logical_not(stays))
        def _():
            pltpu.make_async_remote_copy(
                src_ref=src,
                dst_ref=dst,
                send_sem=mid_send.at[group],
                recv_sem=mid_recv.at[group],
                device_id=(mid_cut, mid_coil),
                device_id_type=MESH,
            ).start()

    def move_out(group):
        planes = pl.ds(FIRST[group], SIZES[group])

        @pl.when(is_mid)
        def _():
            both = mid.at[:, :, planes, :, :]
            pltpu.make_async_copy(both, both, mid_recv.at[group]).wait()

            def one(t, carry):
                part = lax.rem(t, 2)
                x = FIRST[group] + lax.div(t, 2)
                total = mid[0, part, x].astype(F32) + mid[1, part, x].astype(F32)
                osend[part, x] = total.reshape(8, 8, N).astype(BF16)
                return carry

            lax.fori_loop(0, 2 * SIZES[group], one, 0)

            def move(k, carry):
                src = osend.at[:, planes, k, :, :]
                dst = out.at[:, pl.ds(slot * PLANES + FIRST[group], SIZES[group]), :, :]
                itself = jnp.logical_and(keeps, lax.rem(me, 8) == k)

                @pl.when(itself)
                def _():
                    pltpu.make_async_copy(src, dst, mv_recv.at[group]).start()

                @pl.when(jnp.logical_not(itself))
                def _():
                    pltpu.make_async_remote_copy(
                        src_ref=src,
                        dst_ref=dst,
                        send_sem=mv_send.at[group],
                        recv_sem=mv_recv.at[group],
                        device_id=(zlo * 8 + k, owner_coil),
                        device_id_type=MESH,
                    ).start()

                return carry

            lax.fori_loop(0, 8, move, 0)

    for group in range(GROUPS):
        here = arr.at[:, :, pl.ds(FIRST[group], SIZES[group]), :, :, :]
        pltpu.make_async_copy(here, here, a2a_recv.at[group]).wait()
        lax.fori_loop(FIRST[group], FIRST[group] + SIZES[group], back, 0)
        send_sums(group)
        if group > 0:
            finish_sums(group - 1)
    finish_sums(GROUPS - 1)
    for group in range(GROUPS):
        move_out(group)

    for group in range(GROUPS):
        four = out.at[:, pl.ds(0, 4 * SIZES[group]), :, :]
        pltpu.make_async_copy(four, four, mv_recv.at[group]).wait()

    for group in range(GROUPS):
        planes = pl.ds(FIRST[group], SIZES[group])
        sent = hyb.at[:, :, pl.ds(0, 31 * SIZES[group]), :, :]
        pltpu.make_async_copy(sent, sent, a2a_send.at[group]).wait()
        three = rsbuf.at[pl.ds(0, 3), :, planes, :, :]
        pltpu.make_async_copy(three, three, rs_send.at[group]).wait()

        @pl.when(jnp.logical_not(stays))
        def _():
            part = psend.at[:, planes, :, :]
            pltpu.make_async_copy(part, part, mid_send.at[group]).wait()

        @pl.when(jnp.logical_and(is_mid, keeps))
        def _():
            seven = osend.at[:, planes, pl.ds(0, 7), :, :]
            pltpu.make_async_copy(seven, seven, mv_send.at[group]).wait()

        @pl.when(jnp.logical_and(is_mid, jnp.logical_not(keeps)))
        def _():
            eight = osend.at[:, planes, :, :, :]
            pltpu.make_async_copy(eight, eight, mv_send.at[group]).wait()

    seven = vol.at[:, :, pl.ds(0, 224), :]
    pltpu.make_async_copy(seven, seven, ag_send).wait()


def body(volume, coil_maps, kspace, line_mask):
    cos_table, sin_table = tables()
    any_space = pl.BlockSpec(memory_space=pl.ANY)
    dma = pltpu.SemaphoreType.DMA
    return pl.pallas_call(
        kernel,
        out_shape=jax.ShapeDtypeStruct((2, 32, 8, N), BF16),
        in_specs=[any_space] * 6,
        out_specs=any_space,
        scratch_shapes=[
            pltpu.VMEM((2, 2, N, 8, N), BF16),
            pltpu.VMEM((2, 2, PLANES, N, N), BF16),
            pltpu.VMEM((N, N), jnp.int32),
            pltpu.VMEM((2, PLANES, N, N), BF16),
            pltpu.VMEM((N, N), BF16),
            pltpu.VMEM((N, N), BF16),
            pltpu.VMEM((2 * N, 2 * N), BF16),
            pltpu.VMEM((2 * N, 2 * N), BF16),
            pltpu.VMEM((2, 2, 8 * N, 128), F32),
            pltpu.VMEM((2, 2, 8 * N, 128), F32),
            pltpu.VMEM((2, 2, N, 8, N), BF16),
            pltpu.VMEM((2, 2, PLANES, CUTS, 8, N), BF16),
            pltpu.VMEM((2, PLANES, 2 * N, N), BF16),
            pltpu.VMEM((2, PLANES, N, N), BF16),
            pltpu.VMEM((4, 2, PLANES, 64, N), BF16),
            pltpu.VMEM((2, PLANES, 64, N), BF16),
            pltpu.VMEM((2, 2, PLANES, 64, N), BF16),
            pltpu.VMEM((2, PLANES, 8, 8, N), BF16),
            pltpu.VMEM((2, 32, 8, N), BF16),
            dma((6,)),
            dma,
            dma,
            dma,
            dma,
            dma((GROUPS,)),
            dma((GROUPS,)),
            dma((GROUPS,)),
            dma((GROUPS,)),
            dma((GROUPS,)),
            dma((GROUPS,)),
            dma((GROUPS,)),
            dma((GROUPS,)),
            dma,
        ],
        compiler_params=pltpu.CompilerParams(
            collective_id=0, has_side_effects=True, vmem_limit_bytes=60 * 1024 * 1024
        ),
    )(volume, coil_maps, kspace, line_mask, jnp.asarray(cos_table), jnp.asarray(sin_table))


def solution(mesh):
    return jax.shard_map(
        body,
        mesh=mesh,
        in_specs=(
            P(None, "cuts", "coil", None),
            P("coil", None, "cuts", None, None),
            P("coil", None, None, "cuts", None),
            P(),
        ),
        out_specs=P(None, "coil", "cuts", None),
        check_vma=False,
    )
```

```python
import math

import jax
import jax.numpy as jnp
import numpy as np
from jax import lax
from jax.experimental import pallas as pl
from jax.experimental.pallas import tpu as pltpu
from jax.sharding import PartitionSpec as P

MESH = pl.DeviceIdType.MESH
BF16 = jnp.bfloat16
F32 = jnp.float32
N = 256
CUTS = 32
PLANES = 8
SIZES = (3, 3, 1, 1)
GROUPS = len(SIZES)
FIRST = tuple(sum(SIZES[:g]) for g in range(GROUPS))


def tables():
    counter = np.arange(N, dtype=np.int32)
    product = counter[:, None] * counter[None, :] % N
    angles = product.astype(np.float32) * np.float32(2.0 * math.pi / N)
    factor = np.float32(1.0 / math.sqrt(N))
    return (
        (np.cos(angles) * factor).astype(BF16),
        (np.sin(angles) * factor).astype(BF16),
    )


def dot(a, b):
    return jnp.dot(a, b, preferred_element_type=F32)


def kernel(
    vol_in, maps_in, ks_in, mask_in, cos_in, sin_in, out,
    ks, maps, mask, vol, cosv, sinv, fwd, inv, split, merge, hyb, arr, kspc, gsend, rsbuf, psend, mid, osend, fin,
    in_sem, vol_sem, agz_recv, agx_recv, ag_send, a2a_send, a2a_recv, rs_send, rs_recv, mid_send, mid_recv, mv_send, mv_recv, out_sem,
):
    me = lax.axis_index("cuts")
    my_coil = lax.axis_index("coil")
    zhi = lax.div(my_coil, 4)
    xpos = lax.rem(my_coil, 4)
    partner = lax.rem(my_coil + 4, 8)
    zlo = lax.div(me, 8)
    ypos = lax.rem(lax.div(me, 2), 4)
    core = lax.rem(me, 2)
    slot = lax.rem(me, 4)
    shift = lax.rem(zlo + 2 * core, 4)
    quarter = lax.rem(xpos + shift, 4)
    mid_cut = quarter * 8 + lax.rem(me, 8)
    mid_coil = lax.div(zlo, 2) * 4 + xpos
    stays = jnp.logical_and(mid_cut == me, mid_coil == my_coil)
    zlo_from = lax.rem(zlo + 8 - xpos - 2 * core, 4)
    is_mid = lax.div(zlo_from, 2) == zhi
    owner_coil = zlo_from * 2 + lax.div(ypos, 2)
    keeps = owner_coil == my_coil
    zlo_home = 2 * zhi + lax.div(xpos, 2)

    def load(k, src, dst):
        return pltpu.make_async_copy(src, dst, in_sem.at[k])

    loads = [
        load(0, cos_in, cosv),
        load(1, sin_in, sinv),
        load(2, ks_in.at[0], ks.at[0]),
        load(3, ks_in.at[1], ks.at[1]),
        load(4, mask_in, mask),
        load(5, maps_in, maps),
    ]
    for item in loads:
        item.start()
    my_rows = pl.ds(pl.multiple_of(my_coil * 32, 32), 32)
    vol_own = pltpu.make_async_copy(vol_in, vol.at[:, :, my_rows, :], vol_sem)
    vol_own.start()

    barrier = pltpu.get_barrier_semaphore()

    def greet(a, b):
        pl.semaphore_signal(barrier, inc=1, device_id=(a, b), device_id_type=MESH)

    def greet_cut(k, carry):
        greet(lax.rem(me + k, CUTS), my_coil)
        return carry

    lax.fori_loop(1, CUTS, greet_cut, 0)
    greet(me, partner)
    for d in range(1, 4):
        greet(me, zhi * 4 + lax.rem(xpos + d, 4))

    @pl.when(is_mid)
    def _():
        for z in range(2):
            a, b = zlo_from * 8 + lax.rem(me, 8), z * 4 + xpos

            @pl.when(jnp.logical_or(a != me, b != my_coil))
            def _():
                greet(a, b)

    for m in range(4):
        a = zlo * 8 + lax.rem(xpos, 2) * 4 + m
        b = zhi * 4 + lax.rem(zlo + 8 - zlo_home - 2 * (m % 2), 4)

        @pl.when(jnp.logical_or(a != me, b != my_coil))
        def _():
            greet(a, b)

    loads[0].wait()
    loads[1].wait()
    c = cosv[...]
    s = sinv[...]
    fwd[:N, :N] = c
    fwd[N:, N:] = c
    fwd[:N, N:] = -s
    fwd[N:, :N] = s
    inv[:N, :N] = c
    inv[N:, N:] = c
    inv[:N, N:] = s
    inv[N:, :N] = -s

    def transform_x(coil):
        for part in range(2):

            def spread(b, carry):
                v = ks[coil, part, pl.ds(pl.multiple_of(b * 32, 32), 32)].astype(F32).reshape(N, N)
                rows = pl.ds(pl.multiple_of(b * N, N), N)
                split[part, 0, rows, :] = v[:, :128]
                split[part, 1, rows, :] = v[:, 128:]
                return carry

            lax.fori_loop(0, 8, spread, 0)

        def line(ky, carry):
            rows = pl.ds(ky, N, stride=8)
            cols = [
                jnp.concatenate([split[0, half, rows, :], split[1, half, rows, :]], axis=0).astype(BF16)
                for half in range(2)
            ]
            r = dot(fwd[...], jnp.concatenate(cols, axis=1))
            for part in range(2):
                for half in range(2):
                    merge[part, half, rows, :] = r[part * N : (part + 1) * N, half * 128 : (half + 1) * 128]
            return carry

        lax.fori_loop(0, 8, line, 0)
        for part in range(2):

            def gather(b, carry):
                rows = pl.ds(pl.multiple_of(b * N, N), N)
                v = jnp.concatenate([merge[part, 0, rows, :], merge[part, 1, rows, :]], axis=1)
                hyb[coil, part, pl.ds(pl.multiple_of(b * 32, 32), 32)] = v.reshape(32, 8, N).astype(BF16)
                return carry

            lax.fori_loop(0, 8, gather, 0)

    def send_slabs(coil, group):
        planes = pl.ds(FIRST[group], SIZES[group])

        def one(k, carry):
            to = lax.rem(me + k, CUTS)
            pltpu.make_async_remote_copy(
                src_ref=hyb.at[coil, :, pl.ds(to * PLANES + FIRST[group], SIZES[group]), :, :],
                dst_ref=arr.at[coil, :, planes, me, :, :],
                send_sem=a2a_send.at[group],
                recv_sem=a2a_recv.at[group],
                device_id=(to, my_coil),
                device_id_type=MESH,
            ).start()
            return carry

        lax.fori_loop(1, CUTS, one, 0)
        pltpu.make_async_copy(
            hyb.at[coil, :, pl.ds(me * PLANES + FIRST[group], SIZES[group]), :, :],
            arr.at[coil, :, planes, me, :, :],
            a2a_recv.at[group],
        ).start()

    def send_volume(rows, source, peer, recv):
        pltpu.make_async_remote_copy(
            src_ref=source,
            dst_ref=vol.at[:, :, rows, :],
            send_sem=ag_send,
            recv_sem=recv,
            device_id=(me, peer),
            device_id_type=MESH,
        ).start()

    loads[2].wait()
    transform_x(0)
    greeted = jnp.where(is_mid, 8 - keeps.astype(jnp.int32), 0) + 1 - stays.astype(jnp.int32)
    pl.semaphore_wait(barrier, 35 + greeted)

    send_volume(my_rows, vol_in, partner, agz_recv)
    for d in (2, 1, 3):
        send_volume(my_rows, vol_in, zhi * 4 + lax.rem(xpos + d, 4), agx_recv)
    send_slabs(0, 0)
    loads[3].wait()
    transform_x(1)
    send_slabs(1, 0)
    pltpu.make_async_copy(vol_in, vol_in, agz_recv).wait()
    far_rows = pl.ds(pl.multiple_of(partner * 32, 32), 32)
    for d in (2, 1, 3):
        send_volume(far_rows, vol.at[:, :, far_rows, :], zhi * 4 + lax.rem(xpos + d, 4), agx_recv)
    for group in range(1, GROUPS):
        send_slabs(0, group)
        send_slabs(1, group)

    loads[5].wait()
    vol_own.wait()
    six = vol.at[:, :, pl.ds(0, 192), :]
    pltpu.make_async_copy(six, six, agx_recv).wait()

    def predict(t, carry):
        coil = lax.div(t, PLANES)
        x = lax.rem(t, PLANES)
        vr = vol[0, x].astype(F32)
        vi = vol[1, x].astype(F32)
        mr = maps[coil, 0, x].astype(F32)
        mi = maps[coil, 1, x].astype(F32)
        image = jnp.concatenate([(mr * vr - mi * vi).astype(BF16), (mr * vi + mi * vr).astype(BF16)], axis=1)
        z = dot(image, fwd[...]).astype(BF16)
        kspc[coil, x] = dot(inv[...], jnp.concatenate([z[:, :N], z[:, N:]], axis=0)).astype(BF16)
        return carry

    lax.fori_loop(0, 2 * PLANES, predict, 0)
    loads[4].wait()

    def back(x, carry):
        weight = mask[...].astype(F32)
        gr = None
        for coil in range(2):
            res = []
            for part in range(2):
                k = kspc[coil, x, part * N : (part + 1) * N, :].astype(F32)
                h = arr[coil, part, x].astype(F32).reshape(N, N)
                res.append((weight * (k - h)).astype(BF16))
            y = dot(fwd[...], jnp.concatenate(res, axis=0)).astype(BF16)
            b = dot(jnp.concatenate([y[:N], y[N:]], axis=1), inv[...]).astype(BF16).astype(F32)
            br, bi = b[:, :N], b[:, N:]
            mr = maps[coil, 0, x].astype(F32)
            mi = maps[coil, 1, x].astype(F32)
            tr = mr * br + mi * bi
            ti = mr * bi - mi * br
            gr, gi = (tr, ti) if gr is None else (gr + tr, gi + ti)
        gsend[0, x] = (-0.5 * gr).astype(BF16)
        gsend[1, x] = (-0.5 * gi).astype(BF16)
        return carry

    def send_sums(group):
        planes = pl.ds(FIRST[group], SIZES[group])
        for d in (2, 1, 3):
            to = lax.rem(xpos + d, 4)
            pltpu.make_async_remote_copy(
                src_ref=gsend.at[:, planes, pl.ds(pl.multiple_of(lax.rem(to + shift, 4) * 64, 64), 64), :],
                dst_ref=rsbuf.at[xpos, :, planes, :, :],
                send_sem=rs_send.at[group],
                recv_sem=rs_recv.at[group],
                device_id=(me, zhi * 4 + to),
                device_id_type=MESH,
            ).start()

    lead = (1 - zhi).astype(F32)
    own_rows = pl.ds(pl.multiple_of(quarter * 64, 64), 64)

    def finish_sums(group):
        planes = pl.ds(FIRST[group], SIZES[group])
        three = rsbuf.at[pl.ds(0, 3), :, planes, :, :]
        pltpu.make_async_copy(three, three, rs_recv.at[group]).wait()

        def one(t, carry):
            part = lax.rem(t, 2)
            x = FIRST[group] + lax.div(t, 2)
            total = lead * vol[part, x, own_rows, :].astype(F32) + gsend[part, x, own_rows, :].astype(F32)
            for d in range(1, 4):
                total += rsbuf[lax.rem(xpos + d, 4), part, x].astype(F32)
            psend[part, x] = total.astype(BF16)
            return carry

        lax.fori_loop(0, 2 * SIZES[group], one, 0)
        src = psend.at[:, planes, :, :]
        dst = mid.at[zhi, :, planes, :, :]

        @pl.when(stays)
        def _():
            pltpu.make_async_copy(src, dst, mid_recv.at[group]).start()

        @pl.when(jnp.logical_not(stays))
        def _():
            pltpu.make_async_remote_copy(
                src_ref=src,
                dst_ref=dst,
                send_sem=mid_send.at[group],
                recv_sem=mid_recv.at[group],
                device_id=(mid_cut, mid_coil),
                device_id_type=MESH,
            ).start()

    def move_out(group):
        planes = pl.ds(FIRST[group], SIZES[group])

        @pl.when(is_mid)
        def _():
            both = mid.at[:, :, planes, :, :]
            pltpu.make_async_copy(both, both, mid_recv.at[group]).wait()

            def one(t, carry):
                part = lax.rem(t, 2)
                x = FIRST[group] + lax.div(t, 2)
                total = mid[0, part, x].astype(F32) + mid[1, part, x].astype(F32)
                osend[part, x] = total.reshape(8, 8, N).astype(BF16)
                return carry

            lax.fori_loop(0, 2 * SIZES[group], one, 0)

            def move(k, carry):
                src = osend.at[:, planes, k, :, :]
                dst = out.at[:, pl.ds(slot * PLANES + FIRST[group], SIZES[group]), :, :]
                itself = jnp.logical_and(keeps, lax.rem(me, 8) == k)

                @pl.when(itself)
                def _():
                    pltpu.make_async_copy(src, dst, mv_recv.at[group]).start()

                @pl.when(jnp.logical_not(itself))
                def _():
                    pltpu.make_async_remote_copy(
                        src_ref=src,
                        dst_ref=dst,
                        send_sem=mv_send.at[group],
                        recv_sem=mv_recv.at[group],
                        device_id=(zlo * 8 + k, owner_coil),
                        device_id_type=MESH,
                    ).start()

                return carry

            lax.fori_loop(0, 8, move, 0)

    for group in range(GROUPS):
        here = arr.at[:, :, pl.ds(FIRST[group], SIZES[group]), :, :, :]
        pltpu.make_async_copy(here, here, a2a_recv.at[group]).wait()
        lax.fori_loop(FIRST[group], FIRST[group] + SIZES[group], back, 0)
        send_sums(group)
        if group > 0:
            finish_sums(group - 1)
    finish_sums(GROUPS - 1)
    for group in range(GROUPS):
        move_out(group)

    for group in range(GROUPS):
        four = out.at[:, pl.ds(0, 4 * SIZES[group]), :, :]
        pltpu.make_async_copy(four, four, mv_recv.at[group]).wait()

    for group in range(GROUPS):
        planes = pl.ds(FIRST[group], SIZES[group])
        sent = hyb.at[:, :, pl.ds(0, 31 * SIZES[group]), :, :]
        pltpu.make_async_copy(sent, sent, a2a_send.at[group]).wait()
        three = rsbuf.at[pl.ds(0, 3), :, planes, :, :]
        pltpu.make_async_copy(three, three, rs_send.at[group]).wait()

        @pl.when(jnp.logical_not(stays))
        def _():
            part = psend.at[:, planes, :, :]
            pltpu.make_async_copy(part, part, mid_send.at[group]).wait()

        @pl.when(jnp.logical_and(is_mid, keeps))
        def _():
            seven = osend.at[:, planes, pl.ds(0, 7), :, :]
            pltpu.make_async_copy(seven, seven, mv_send.at[group]).wait()

        @pl.when(jnp.logical_and(is_mid, jnp.logical_not(keeps)))
        def _():
            eight = osend.at[:, planes, :, :, :]
            pltpu.make_async_copy(eight, eight, mv_send.at[group]).wait()

    seven = vol.at[:, :, pl.ds(0, 224), :]
    pltpu.make_async_copy(seven, seven, ag_send).wait()


def body(volume, coil_maps, kspace, line_mask):
    cos_table, sin_table = tables()
    any_space = pl.BlockSpec(memory_space=pl.ANY)
    dma = pltpu.SemaphoreType.DMA
    return pl.pallas_call(
        kernel,
        out_shape=jax.ShapeDtypeStruct((2, 32, 8, N), BF16),
        in_specs=[any_space] * 6,
        out_specs=any_space,
        scratch_shapes=[
            pltpu.VMEM((2, 2, N, 8, N), BF16),
            pltpu.VMEM((2, 2, PLANES, N, N), BF16),
            pltpu.VMEM((N, N), jnp.int32),
            pltpu.VMEM((2, PLANES, N, N), BF16),
            pltpu.VMEM((N, N), BF16),
            pltpu.VMEM((N, N), BF16),
            pltpu.VMEM((2 * N, 2 * N), BF16),
            pltpu.VMEM((2 * N, 2 * N), BF16),
            pltpu.VMEM((2, 2, 8 * N, 128), F32),
            pltpu.VMEM((2, 2, 8 * N, 128), F32),
            pltpu.VMEM((2, 2, N, 8, N), BF16),
            pltpu.VMEM((2, 2, PLANES, CUTS, 8, N), BF16),
            pltpu.VMEM((2, PLANES, 2 * N, N), BF16),
            pltpu.VMEM((2, PLANES, N, N), BF16),
            pltpu.VMEM((4, 2, PLANES, 64, N), BF16),
            pltpu.VMEM((2, PLANES, 64, N), BF16),
            pltpu.VMEM((2, 2, PLANES, 64, N), BF16),
            pltpu.VMEM((2, PLANES, 8, 8, N), BF16),
            pltpu.VMEM((2, 32, 8, N), BF16),
            dma((6,)),
            dma,
            dma,
            dma,
            dma,
            dma((GROUPS,)),
            dma((GROUPS,)),
            dma((GROUPS,)),
            dma((GROUPS,)),
            dma((GROUPS,)),
            dma((GROUPS,)),
            dma((GROUPS,)),
            dma((GROUPS,)),
            dma,
        ],
        compiler_params=pltpu.CompilerParams(
            collective_id=0, has_side_effects=True, vmem_limit_bytes=60 * 1024 * 1024
        ),
    )(volume, coil_maps, kspace, line_mask, jnp.asarray(cos_table), jnp.asarray(sin_table))


def solution(mesh):
    return jax.shard_map(
        body,
        mesh=mesh,
        in_specs=(
            P(None, "cuts", "coil", None),
            P("coil", None, "cuts", None, None),
            P("coil", None, None, "cuts", None),
            P(),
        ),
        out_specs=P(None, "coil", "cuts", None),
        check_vma=False,
    )
```
